32 devices in a mesh: tm: 4 (over x, core), row: 8 (over z, y).
Axes of the slice: x: 2, y: 2, z: 4, core: 2. Of those that a mesh axis runs over, the one named last changes fastest.
Arguments:
- image: float32 [4, 1, 512, 2048], P('tm', None, 'row'), may hold values from -6 to 6
- relaxed: float32 [4, 1, 512, 2048], P('tm', None, 'row'), may hold values from -6 to 6
- dual: float32 [4, 1, 512, 2048], P('tm', None, 'row'), may hold values from -2 to 2
- sinogram: float32 [4, 12, 1, 2048], P('tm'), may hold values from -48 to 48
- angle_index: int32 [4, 12], P('tm'), may hold values from 0 to 31, as said below
- bin_offset: int32 [32, 32], P('row'), may hold values from 0 to 2047
- row_weight: float32 [32, 16], replicated, may hold values from 0.5 to 1.5
- response: bfloat16 [32, 128, 128], replicated, may hold values from -0.5 to 0.5
- row_gain: float32 [512], P('row'), may hold values from 0.6 to 11.2
Outputs:
- image_new: float32 [4, 1, 512, 2048], P('tm', None, 'row')
- dual_new: float32 [4, 1, 512, 2048], P('tm', None, 'row')
The draws below stay inside these ranges and needn't reach their ends.
Inputs may be any that keep to these rules, and one draw needn't show every extreme that they name: `angle_index`: the 12 views of one phase name distinct entries of the angle table.
All inputs are finite; a program needn't handle non-finite values.
Results may differ from the reference program's by a relative error of at most 0.0003.
Values sent between devices are 32-bit elements; how exact they have to be, the bound alone decides.
No kernel may reach another device: no remote copies, remote signals or barrier semaphores. Data moves between devices by JAX's collectives and lax.ppermute only.
A program may use at most 64 MiB of HBM per device.

```python
import jax
import jax.numpy as jnp
from jax import lax

COLS = 2048
BLK = 128
SLICES = 1
TR = 16
VIEWS = 12
NANG = 32
CG_ITERS = 3
PHASES = 4
ROWS = 512
TILES = 32


def draw_angle_index(key, part):
    keys = jax.random.split(jax.random.fold_in(key, 11), PHASES)

    def order(single):
        return jax.random.permutation(single, NANG)
    orders = jax.vmap(order)(keys)
    return orders[:, :VIEWS].astype(jnp.int32)


def draw_row_gain(key, part):
    position = jnp.arange(ROWS, dtype=jnp.float32) / float(max(ROWS - 1, 1))
    rough = jax.random.uniform(jax.random.fold_in(key, 23), (ROWS,), jnp.float32, 0.6, 1.4)
    rising = 4.0
    return (jnp.exp(jnp.log(rising) * position) * rough).astype(jnp.float32)


def plant(values, key, low, largest):
    longest = values.shape.index(max(values.shape))
    spots = []
    for shift in (0, 1):
        where = [jax.random.randint(jax.random.fold_in(key, axis), (), 0, length) for axis, length in enumerate(values.shape)]
        where[longest] = (where[longest] + shift) % values.shape[longest]
        spots.append(tuple(where))
    return values.at[spots[0]].set(low).at[spots[1]].set(largest)


def block_scale(stream_key, shape, cuts, low, high):
    level, own = 1.0, jax.random.fold_in(stream_key, 6)
    for dim, shards_of in cuts:
        heights = jnp.exp(jax.random.uniform(jax.random.fold_in(own, dim), (shards_of,), jnp.float32, low / len(cuts), high / len(cuts)))
        level = level * jnp.repeat(heights, shape[dim] // shards_of).reshape([-1 if axis == dim else 1 for axis in range(len(shape))])
    return level


def noise(stream_key, shape, deviation, bound, cuts=(), held_as=jnp.bfloat16):
    drawn = jax.random.normal(stream_key, shape, jnp.float32) * deviation
    if len(cuts) > 0:
        drawn = block_scale(stream_key, shape, cuts, -0.22, 0.18) * drawn
    return jnp.clip(drawn, min=-bound, max=bound).astype(held_as)


def setup_inputs(seed: int = 0) -> dict:
    arg_keys = jax.random.split(jax.random.key(seed), 10)
    return {
        "image": noise(arg_keys[0], (PHASES, SLICES, ROWS, COLS), 1.0, 6.0, ((0, 4), (2, 8)), jnp.float32),
        "relaxed": noise(arg_keys[1], (PHASES, SLICES, ROWS, COLS), 1.0, 6.0, ((0, 4), (2, 8)), jnp.float32),
        "dual": jnp.clip(jax.random.uniform(arg_keys[2], (PHASES, SLICES, ROWS, COLS), jnp.float32, -2.0, 2.0) * block_scale(arg_keys[2], (PHASES, SLICES, ROWS, COLS), ((0, 4), (2, 8)), -0.4, 0.0), -2.0, 2.0),
        "sinogram": noise(arg_keys[3], (PHASES, VIEWS, SLICES, COLS), 8.0, 48.0, ((0, 4),), jnp.float32),
        "angle_index": draw_angle_index(jax.random.fold_in(arg_keys[9], 71), 0),
        "bin_offset": plant(jax.random.randint(arg_keys[5], (TILES, NANG), 0, COLS), jax.random.fold_in(arg_keys[5], 1), 0, COLS - 1).astype(jnp.int32),
        "row_weight": jnp.clip(jax.random.uniform(arg_keys[6], (NANG, TR), jnp.float32, 0.5, 1.5), 0.5, 1.5),
        "response": noise(arg_keys[7], (NANG, BLK, BLK), BLK ** -0.5, 0.5),
        "row_gain": draw_row_gain(jax.random.fold_in(arg_keys[9], 71), 0),
    }


HIGH = lax.Precision.HIGHEST
TAU_STEP = 0.1
SIGMA_STEP = 2.0
LAMBDA_BOUND = 2.0


def view_tables(angles, row_weight, response, bin_offset):
    selector = angles[:, None] == jnp.arange(row_weight.shape[0], dtype=jnp.int32)[None, :]
    chosen = selector.astype(jnp.float32)
    weights = jnp.dot(chosen, row_weight, precision=HIGH)
    blocks = jnp.einsum('va,aio->vio', chosen, response.astype(jnp.float32), precision=HIGH)
    shifts = jnp.sum(jnp.where(selector[None, :, :], bin_offset[:, None, :], 0), axis=2).astype(jnp.int32)
    return weights, blocks, shifts


def shift_columns(rows, start):
    width = rows.shape[-1]
    doubled = jnp.concatenate([rows, rows], axis=-1)
    return lax.dynamic_slice_in_dim(doubled, start.astype(jnp.int32), width, axis=rows.ndim - 1)


def spread_view(rows, starts):
    width = rows.shape[-1]
    doubled = jnp.concatenate([rows, rows], axis=-1)

    def pick(start):
        return lax.dynamic_slice_in_dim(doubled, start.astype(jnp.int32), width, axis=rows.ndim - 1)

    return jax.vmap(pick)(starts)


def project(volume, weights, blocks, shifts):
    num_slices, num_rows, num_cols = volume.shape
    num_views, tile_rows = weights.shape
    block_width = blocks.shape[1]
    tile_count = num_rows // tile_rows
    tiled = volume.reshape(num_slices, tile_count, tile_rows, num_cols)
    summed = jnp.einsum('vj,skjc->vksc', weights, tiled, precision=HIGH)
    blocked = summed.reshape(num_views, tile_count, num_slices, num_cols // block_width, block_width)
    mapped = jnp.einsum('vksni,vio->vksno', blocked, blocks, precision=HIGH)
    mapped = mapped.reshape(num_views, tile_count, num_slices, num_cols)
    starts = ((num_cols - jnp.transpose(shifts)) % num_cols).astype(jnp.int32)
    rolled = jax.vmap(jax.vmap(shift_columns))(mapped, starts)
    return jnp.sum(rolled, axis=1)


def backproject(projected, weights, blocks, shifts):
    num_views, num_slices, num_cols = projected.shape
    tile_rows = weights.shape[1]
    block_width = blocks.shape[1]
    tile_count = shifts.shape[0]
    starts = (jnp.transpose(shifts) % num_cols).astype(jnp.int32)
    picked = jax.vmap(spread_view)(projected, starts)
    blocked = picked.reshape(num_views, tile_count, num_slices, num_cols // block_width, block_width)
    mapped = jnp.einsum('vksno,vio->vksni', blocked, blocks, precision=HIGH)
    mapped = mapped.reshape(num_views, tile_count, num_slices, num_cols)
    tiled = jnp.einsum('vj,vksc->skjc', weights, mapped, precision=HIGH)
    return tiled.reshape(num_slices, tile_count * tile_rows, num_cols)


def reference(image, relaxed, dual, sinogram, angle_index, bin_offset, row_weight, response, row_gain):
    dual_new = jnp.clip(dual + SIGMA_STEP * (jnp.roll(relaxed, -1, axis=0) - relaxed), -LAMBDA_BOUND, LAMBDA_BOUND)
    primal = image - TAU_STEP * (jnp.roll(dual_new, 1, axis=0) - dual_new)
    gain = row_gain[None, :, None]

    def solve_phase(inputs):
        start, measured, angles = inputs
        weights, blocks, shifts = view_tables(angles, row_weight, response, bin_offset)

        def forward(volume):
            return project(volume * gain, weights, blocks, shifts)

        def adjoint(projected):
            return backproject(projected, weights, blocks, shifts) * gain

        def normal(direction):
            return adjoint(forward(direction)) + direction / TAU_STEP

        solution = start
        resid = adjoint(measured - forward(start))
        direction = resid
        norm_now = jnp.sum(resid * resid)
        for step in range(CG_ITERS):
            image_w = normal(direction)
            alpha = norm_now / jnp.sum(direction * image_w)
            solution = solution + alpha * direction
            resid = resid - alpha * image_w
            norm_next = jnp.sum(resid * resid)
            direction = resid + (norm_next / norm_now) * direction
            norm_now = norm_next
        return solution

    image_new = lax.map(solve_phase, (primal, sinogram, angle_index))
    return image_new, dual_new
```

```python
import functools

import jax
import jax.numpy as jnp
from jax import lax
from jax.experimental import pallas as pl
from jax.experimental.pallas import tpu as pltpu
from jax.sharding import PartitionSpec as P

CG_ITERS = 3
TAU_STEP = 0.1
SIGMA_STEP = 2.0
LAMBDA_BOUND = 2.0
HIGH = lax.Precision.HIGHEST
LANES = 128


def halves(x):
    high = x.astype(jnp.bfloat16)
    low = (x - high.astype(jnp.float32)).astype(jnp.bfloat16)
    return high, low


def lane_index(rows):
    return lax.broadcasted_iota(jnp.int32, (rows, LANES), 1)


def pull(load, offset, lane):
    block, rest = offset >> 7, offset & (LANES - 1)
    mixed = jnp.where(lane < rest, load(block + 1), load(block))
    return pltpu.roll(mixed, (LANES - rest) & (LANES - 1), 1)


def push(load, offset, lane, blocks):
    block, rest = offset >> 7, offset & (LANES - 1)
    mixed = jnp.where(lane >= LANES - rest, load(blocks - 1 - block), load(blocks - block))
    return pltpu.roll(mixed, rest, 1)


def project_sets(stack, tables, zs, ep, hd, tiles, views, blocks):
    lane = lane_index(blocks)
    rows = tiles * blocks
    total = stack.shape[0]
    for b in range(blocks):
        zs[pl.ds(b, total, stride=blocks), :] = stack[:, b * LANES : (b + 1) * LANES]
    for s, (response, offsets, out, init) in enumerate(tables):
        for v in range(views):
            at = (s * views + v) * rows
            slot = v % 2
            high, low = halves(zs[at : at + rows, :])
            ep[slot, :, :LANES] = high
            ep[slot, :, LANES:] = low
            h = jnp.dot(ep[slot], response[v], preferred_element_type=jnp.float32)
            h = h.reshape(tiles, blocks, LANES)
            hd[slot, :, :blocks, :] = h
            hd[slot, :, blocks:, :] = h
            total_v = None if init is None else init[v * blocks : (v + 1) * blocks, :]
            for k in range(tiles):
                part = push(
                    lambda q: hd[slot, k, pl.ds(q, blocks), :], offsets[k * views + v], lane, blocks
                )
                total_v = part if total_v is None else total_v + part
            out[v * blocks : (v + 1) * blocks, :] = total_v


def project_scratch(sets, tiles, views, blocks):
    return [
        pltpu.VMEM((sets * views * tiles * blocks, LANES), jnp.float32),
        pltpu.VMEM((2, tiles * blocks, 2 * LANES), jnp.bfloat16),
        pltpu.VMEM((2, tiles, 2 * blocks, LANES), jnp.float32),
    ]


def image_kernel(offs, image, weights, response, out, zs, ep, hd, *, tiles, views, blocks):
    stack = jnp.dot(weights[...], image[...], precision=HIGH, preferred_element_type=jnp.float32)
    project_sets(stack, [(response, offs, out, None)], zs, ep, hd, tiles, views, blocks)


def dual_kernel(
    offs_own, offs_next, dual, relaxed, ahead, weights, resp_own, resp_next, before, table,
    dual_new, msg_own, msg_next, zs, ep, hd, *, tiles, views, blocks,
):
    fresh = jnp.clip(
        dual[...] + SIGMA_STEP * (ahead[...] - relaxed[...]), -LAMBDA_BOUND, LAMBDA_BOUND
    )
    dual_new[...] = fresh
    stack = jnp.dot(weights[...], fresh, precision=HIGH, preferred_element_type=jnp.float32)
    project_sets(
        stack,
        [(resp_own, offs_own, msg_own, before), (resp_next, offs_next, msg_next, None)],
        zs, ep, hd, tiles, views, blocks,
    )
    size = views * blocks
    msg_own[size:, :] = table[...]


def cg_kernel(
    tab, offs, meas, acc0, acc1, resp, resp_t, spread,
    out, y, d, gd, gy, step, wd, ep, f, z2, hd, fs,
    *, tiles, views, blocks, devices, chunk, table_rows, off_row,
):
    lane = lane_index(blocks)
    chunks = devices // chunk
    chunk_tiles = chunk * tiles
    rows = chunk_tiles * blocks

    def view_rows(v):
        return pl.ds(pl.multiple_of(v * blocks, blocks), blocks)

    def double(src):
        whole = src.reshape(views, blocks, LANES)
        wd[:, :blocks, :] = whole
        wd[:, blocks:, :] = whole

    def offset_of(device, k, v):
        return tab[device * table_rows + off_row, k * views + v].astype(jnp.int32)

    def apply():
        def spread_view(at, carry):
            c, v = at // views, at % views
            for i in range(chunk_tiles):
                offset = offset_of(c * chunk + i // tiles, i % tiles, v)
                e = pull(lambda q: wd[v, pl.ds(q, blocks), :], offset, lane)
                high, low = halves(e)
                ep[i * blocks : (i + 1) * blocks, :LANES] = high
                ep[i * blocks : (i + 1) * blocks, LANES:] = low
            f[c, v] = jnp.dot(ep[...], resp_t[v], preferred_element_type=jnp.float32)
            return carry

        lax.fori_loop(0, chunks * views, spread_view, 0)

        def mix(device, carry):
            c, i0 = device // chunk, (device % chunk) * tiles
            for k in range(tiles):
                here = pl.ds(pl.multiple_of((i0 + k) * blocks, blocks), blocks)
                parts = [f[c, v, here, :] for v in range(views)]
                for w in range(views):
                    total = None
                    for v in range(views):
                        at = (k * views + w) * views + v
                        term = tab[device * table_rows + at // LANES, at % LANES] * parts[v]
                        total = term if total is None else total + term
                    high, low = halves(total)
                    z2[c, w, here, :LANES] = high
                    z2[c, w, here, LANES:] = low
            return carry

        lax.fori_loop(0, devices, mix, 0)

        def gather_view(v, carry):
            total = jnp.zeros((blocks, LANES), jnp.float32)
            for c in range(chunks):
                h = jnp.dot(z2[c, v], resp[v], preferred_element_type=jnp.float32)
                h = h.reshape(chunk_tiles, blocks, LANES)
                hd[:, :blocks, :] = h
                hd[:, blocks:, :] = h
                for i in range(chunk_tiles):
                    offset = offset_of(c * chunk + i // tiles, i % tiles, v)
                    total = total + push(
                        lambda q: hd[i, pl.ds(q, blocks), :], offset, lane, blocks
                    )
            gy[view_rows(v), :] = total
            return carry

        lax.fori_loop(0, views, gather_view, 0)

    first = meas[...] - (acc0[...] + acc1[...])
    y[...] = first
    double(first)
    zero = jnp.zeros_like(first)
    d[...] = zero
    gd[...] = zero
    step[...] = zero

    def iterate(n, norm_before):
        apply()
        new_y, new_gy = y[...], gy[...]
        norm = jnp.sum(new_y * new_gy)
        beta = jnp.where(n == 0, 0.0, norm / norm_before)
        new_d = new_y + beta * d[...]
        new_gd = new_gy + beta * gd[...]
        product = jnp.sum(new_gd * new_gd) + jnp.sum(new_d * new_gd) / TAU_STEP
        alpha = norm / product
        d[...] = new_d
        gd[...] = new_gd
        step[...] = step[...] + alpha * new_d
        new_y = new_y - alpha * (new_gd + new_d / TAU_STEP)
        y[...] = new_y
        double(new_y)
        return norm

    lax.fori_loop(0, CG_ITERS, iterate, jnp.float32(1.0))

    double(step[...])
    own = tiles * blocks
    for v in range(views):
        for k in range(tiles):
            e = pull(lambda q: wd[v, pl.ds(q, blocks), :], offs[k * views + v], lane)
            high, low = halves(e)
            ep[k * blocks : (k + 1) * blocks, :LANES] = high
            ep[k * blocks : (k + 1) * blocks, LANES:] = low
        fs[v * own : (v + 1) * own, :] = jnp.dot(
            ep[:own, :], resp_t[v], preferred_element_type=jnp.float32
        )
    for b in range(blocks):
        picked = fs[pl.ds(b, views * tiles, stride=blocks), :]
        out[:, b * LANES : (b + 1) * LANES] = jnp.dot(
            spread[...], picked, precision=HIGH, preferred_element_type=jnp.float32
        )


VMEM = pl.BlockSpec(memory_space=pltpu.VMEM)
SMEM = pl.BlockSpec(memory_space=pltpu.SMEM)


def f32(*shape):
    return jax.ShapeDtypeStruct(shape, jnp.float32)


def exchange(x, sizes, ahead, mask):
    phases, rows = sizes
    pairs = [
        (t * rows + r, ((t + ahead) % phases) * rows + (r ^ mask))
        for t in range(phases)
        for r in range(rows)
    ]
    return lax.ppermute(x, ("tm", "row"), pairs)


def local(image, relaxed, dual, sinogram, angle_index, bin_offset, row_weight, response, row_gain):
    phases, devices = lax.axis_size("tm"), lax.axis_size("row")
    sizes = (phases, devices)
    num_rows, cols = image.shape[2:]
    views = angle_index.shape[1]
    angles = row_weight.shape[0]
    tiles = bin_offset.shape[0]
    tile_rows = row_weight.shape[1]
    blocks = cols // LANES
    size = views * blocks
    image2, relaxed2, dual2 = (a.reshape(num_rows, cols) for a in (image, relaxed, dual))

    ring = [(i, (i - 1) % phases) for i in range(phases)]
    ahead = lax.ppermute(relaxed2, "tm", ring)
    next_angles = lax.ppermute(angle_index, "tm", ring)

    gain = row_gain.reshape(tiles, tile_rows)
    eye = jnp.eye(tiles, dtype=jnp.float32)

    def view_tables(chosen):
        selector = chosen[:, None] == jnp.arange(angles, dtype=jnp.int32)[None, :]
        weights = jnp.dot(selector.astype(jnp.float32), row_weight, precision=HIGH)
        offsets = jnp.sum(jnp.where(selector[None], bin_offset[:, None, :], 0), axis=2)
        blocks_of = jnp.take(response, chosen, axis=0)
        spread = weights[:, None, None, :] * eye[None, :, :, None] * gain[None, None, :, :]
        return weights, offsets, blocks_of, spread.reshape(views * tiles, num_rows)

    weights, offs_own, own, spread_own = view_tables(angle_index[0])
    _, offs_next, following, spread_next = view_tables(next_angles[0])
    own_t = jnp.swapaxes(own, 1, 2)
    resp = jnp.concatenate([own, own], axis=1)
    resp_t = jnp.concatenate([own_t, own_t], axis=1)
    resp_next = jnp.concatenate([following, following], axis=1)
    coupling = jnp.einsum("kj,vj,wj->kvw", gain * gain, weights, weights, precision=HIGH)
    coef_rows = -(-coupling.size // LANES)
    off_rows = -(-offs_own.size // LANES)
    table_rows = -(-(coef_rows + off_rows) // 8) * 8
    table = jnp.concatenate(
        [
            jnp.pad(coupling.reshape(-1), (0, coef_rows * LANES - coupling.size)),
            jnp.pad(
                offs_own.reshape(-1).astype(jnp.float32),
                (0, (table_rows - coef_rows) * LANES - offs_own.size),
            ),
        ]
    ).reshape(table_rows, LANES)
    offs_own = offs_own.reshape(-1)
    offs_next = offs_next.reshape(-1)
    meas = sinogram.reshape(size, LANES)

    dims = dict(tiles=tiles, views=views, blocks=blocks)
    before = pl.pallas_call(
        functools.partial(image_kernel, **dims),
        out_shape=f32(size, LANES),
        in_specs=[SMEM, VMEM, VMEM, VMEM],
        out_specs=VMEM,
        scratch_shapes=project_scratch(1, **dims),
        name="project_image",
    )(offs_own, image2, spread_own, resp)

    both = jnp.concatenate([TAU_STEP * spread_own, -TAU_STEP * spread_next], axis=0)
    dual_new, msg, msg_next = pl.pallas_call(
        functools.partial(dual_kernel, **dims),
        out_shape=(f32(num_rows, cols), f32(size + table_rows, LANES), f32(size, LANES)),
        in_specs=[SMEM, SMEM] + [VMEM] * 8,
        out_specs=(VMEM, VMEM, VMEM),
        scratch_shapes=project_scratch(2, **dims),
        name="dual_project",
    )(offs_own, offs_next, dual2, relaxed2, ahead, both, resp, resp_next, before, table)

    masks = [1 << b if b < 2 else 3 << (b - 1) for b in range(devices.bit_length() - 1)]
    got = exchange(msg, sizes, 0, masks[0])
    got_next = exchange(msg_next, sizes, 1, 0)
    got_cross = exchange(msg_next, sizes, 1, masks[0])
    total = msg[:size] + got[:size] + (got_next + got_cross)
    tables = jnp.concatenate([msg[size:], got[size:]], axis=0)
    other = jnp.zeros_like(total)
    for n, mask in enumerate(masks[1:]):
        got = exchange(jnp.concatenate([total, tables], axis=0), sizes, 0, mask)
        tables = jnp.concatenate([tables, got[size:]], axis=0)
        if n + 2 < len(masks):
            total = total + got[:size]
        else:
            other = got[:size]
    behind = lax.ppermute(dual_new, "tm", [(i, (i + 1) % phases) for i in range(phases)])

    chunk = 1
    while chunk * 2 * tiles <= 32 and devices % (chunk * 2) == 0:
        chunk *= 2
    chunks, rows = devices // chunk, chunk * tiles * blocks
    update = pl.pallas_call(
        functools.partial(
            cg_kernel, **dims, devices=devices, chunk=chunk, table_rows=table_rows, off_row=coef_rows
        ),
        out_shape=f32(num_rows, cols),
        in_specs=[SMEM, SMEM] + [VMEM] * 6,
        out_specs=VMEM,
        scratch_shapes=[pltpu.VMEM((size, LANES), jnp.float32)] * 5
        + [
            pltpu.VMEM((views, 2 * blocks, LANES), jnp.float32),
            pltpu.VMEM((rows, 2 * LANES), jnp.bfloat16),
            pltpu.VMEM((chunks, views, rows, LANES), jnp.float32),
            pltpu.VMEM((chunks, views, rows, 2 * LANES), jnp.bfloat16),
            pltpu.VMEM((chunk * tiles, 2 * blocks, LANES), jnp.float32),
            pltpu.VMEM((views * tiles * blocks, LANES), jnp.float32),
        ],
        name="sinogram_cg",
    )(tables, offs_own, meas, total, other, resp, resp_t, spread_own.T)

    image_new = image2 + TAU_STEP * dual_new - TAU_STEP * behind + update
    return image_new.reshape(image.shape), dual_new.reshape(dual.shape)


def solution(mesh):
    return jax.shard_map(
        local,
        mesh=mesh,
        in_specs=(
            P("tm", None, "row", None),
            P("tm", None, "row", None),
            P("tm", None, "row", None),
            P("tm", None, None, None),
            P("tm", None),
            P("row", None),
            P(),
            P(),
            P("row"),
        ),
        out_specs=(P("tm", None, "row", None), P("tm", None, "row", None)),
        check_vma=False,
    )
```

```python
import functools

import jax
import jax.numpy as jnp
from jax import lax
from jax.experimental import pallas as pl
from jax.experimental.pallas import tpu as pltpu
from jax.sharding import PartitionSpec as P

CG_ITERS = 3
TAU_STEP = 0.1
SIGMA_STEP = 2.0
LAMBDA_BOUND = 2.0
HIGH = lax.Precision.HIGHEST
LANES = 128


def halves(x):
    high = x.astype(jnp.bfloat16)
    low = (x - high.astype(jnp.float32)).astype(jnp.bfloat16)
    return high, low


def product(a, b):
    (ah, al), (bh, bl) = halves(a), halves(b)
    dot = functools.partial(jnp.dot, preferred_element_type=jnp.float32)
    return dot(ah, bh) + (dot(ah, bl) + dot(al, bh))


def lane_index(rows):
    return lax.broadcasted_iota(jnp.int32, (rows, LANES), 1)


def pull(load, offset, lane):
    block, rest = offset >> 7, offset & (LANES - 1)
    mixed = jnp.where(lane < rest, load(block + 1), load(block))
    return pltpu.roll(mixed, (LANES - rest) & (LANES - 1), 1)


def push(load, offset, lane, blocks):
    block, rest = offset >> 7, offset & (LANES - 1)
    mixed = jnp.where(lane >= LANES - rest, load(blocks - 1 - block), load(blocks - block))
    return pltpu.roll(mixed, rest, 1)


def project_sets(stack, bins, tables, zs, hd, tiles, views, blocks):
    lane = lane_index(blocks)
    rows = tiles * blocks
    total = stack.shape[0]
    for b in range(blocks):
        zs[pl.ds(b, total, stride=blocks), :] = stack[:, b * LANES : (b + 1) * LANES]
    for s, (response, angles, out, init) in enumerate(tables):
        for v in range(views):
            at = (s * views + v) * rows
            lhs = jnp.concatenate(halves(zs[at : at + rows, :]), axis=1)
            h = jnp.dot(lhs, response[v], preferred_element_type=jnp.float32)
            for k in range(tiles):
                part = h[k * blocks : (k + 1) * blocks, :]
                hd[2 * at + 2 * k * blocks : 2 * at + (2 * k + 1) * blocks, :] = part
                hd[2 * at + (2 * k + 1) * blocks : 2 * at + (2 * k + 2) * blocks, :] = part
            whole = None if init is None else init[v * blocks : (v + 1) * blocks, :]
            for k in range(tiles):
                part = push(
                    lambda q: hd[pl.ds(2 * at + 2 * k * blocks + q, blocks), :],
                    bins[k, angles[0, v]], lane, blocks,
                )
                whole = part if whole is None else whole + part
            out[v * blocks : (v + 1) * blocks, :] = whole


def project_scratch(sets, tiles, views, blocks):
    rows = sets * views * tiles * blocks
    return [pltpu.VMEM((rows, LANES), jnp.float32), pltpu.VMEM((2 * rows, LANES), jnp.float32)]


def view_tables(angles, weights, gain, response, resp, resp_t, spread, tiles, views):
    width = gain.shape[1]
    row = lax.broadcasted_iota(jnp.int32, (tiles, width), 0)
    column = lax.broadcasted_iota(jnp.int32, (tiles, width), 1) // (width // tiles)
    scale = jnp.where(row == column, jnp.broadcast_to(gain[...], (tiles, width)), 0.0)
    for v in range(views):
        angle = angles[0, v]
        block = response[angle]
        resp[v, :LANES, :] = block
        resp[v, LANES:, :] = block
        if resp_t is not None:
            turned = block.astype(jnp.float32).T.astype(jnp.bfloat16)
            resp_t[v, :LANES, :] = turned
            resp_t[v, LANES:, :] = turned
        spread[v * tiles : (v + 1) * tiles, :] = scale * weights[pl.ds(angle, 1), :]


def tile_weights(weights, tall, tiles):
    width = weights.shape[1]
    for k in range(tiles):
        tall[:, k * width : (k + 1) * width] = weights[...]


def own_kernel(
    angles, bins, image, weights, gain, response,
    resp, resp_t, spread, spread_t, table, before, zs, hd, chosen, tall,
    *, tiles, views, blocks,
):
    tile_weights(weights, tall, tiles)
    view_tables(angles, tall, gain, response, resp, resp_t, spread, tiles, views)
    mine = spread[...]
    spread_t[...] = mine.T
    chosen[...] = jnp.zeros_like(chosen)
    for v in range(views):
        chosen[v : v + 1, :] = tall[pl.ds(angles[0, v], 1), :]
    coupling = lax.dot_general(
        chosen[...], mine * gain[...], (((1,), (1,)), ((), ())),
        precision=HIGH, preferred_element_type=jnp.float32,
    )
    table[...] = jnp.zeros_like(table)
    table[:, : views * tiles] = coupling
    lane = lane_index(8)
    offsets = jnp.zeros((8, LANES), jnp.int32)
    for v in range(views):
        for k in range(tiles):
            offsets = jnp.where(lane == v * tiles + k, bins[k, angles[0, v]], offsets)
    table[views : views + 1, :] = offsets[:1, :].astype(jnp.float32)
    project_sets(
        product(mine, image[...]), bins, [(resp, angles, before, None)],
        zs, hd, tiles, views, blocks,
    )


def next_kernel(angles, weights, gain, response, resp, spread, tall, *, tiles, views):
    tile_weights(weights, tall, tiles)
    view_tables(angles, tall, gain, response, resp, None, spread, tiles, views)


def dual_kernel(
    angles, angles_next, bins, dual, relaxed, ahead, spread, spread_next, resp, resp_next,
    before, table, dual_new, msg_own, msg_next, zs, hd, *, tiles, views, blocks,
):
    fresh = jnp.clip(
        dual[...] + SIGMA_STEP * (ahead[...] - relaxed[...]), -LAMBDA_BOUND, LAMBDA_BOUND
    )
    dual_new[...] = fresh
    both = jnp.concatenate([TAU_STEP * spread[...], -TAU_STEP * spread_next[...]], axis=0)
    project_sets(
        product(both, fresh), bins,
        [(resp, angles, msg_own, before), (resp_next, angles_next, msg_next, None)],
        zs, hd, tiles, views, blocks,
    )
    msg_own[views * blocks :, :] = table[...]


def cg_kernel(
    angles, bins, first, second, meas, resp, resp_t, spread, image, dual_new, behind,
    out, y, d, gd, gy, step, wd, f, z2, hd0, hd1, hd2, hd3, fs, coef, shifts_v, shifts, sem,
    *, tiles, views, blocks, devices, group, table_rows,
):
    hds = (hd0, hd1, hd2, hd3)
    lane = lane_index(blocks)
    size = views * blocks
    half = devices // 2
    per_device = tiles * views
    for n, src in enumerate((first, second)):
        there = src[pl.ds(size + views, half, stride=table_rows), :].astype(jnp.int32)
        back = (blocks * LANES - there) & (blocks * LANES - 1)
        for m, value in enumerate((there >> 7, there & (LANES - 1), back >> 7, back & (LANES - 1))):
            shifts_v[m * devices + n * half : m * devices + (n + 1) * half, :] = value
    to_scalars = pltpu.make_async_copy(shifts_v, shifts, sem)
    to_scalars.start()

    def turn(src, base, device, at, sign):
        mine, other = (0, 2 * devices) if sign > 0 else (2 * devices, 0)
        block = shifts[mine + device, at]
        rest = shifts[mine + devices + device, at]
        back = shifts[other + devices + device, at]
        row = base + block
        mixed = jnp.where(
            lane < rest, src[pl.ds(row + 1, blocks), :], src[pl.ds(row, blocks), :]
        )
        return pltpu.roll(mixed, back, 1)

    def double(src):
        for v in range(views):
            whole = src[v * blocks : (v + 1) * blocks, :]
            wd[2 * v * blocks : (2 * v + 1) * blocks, :] = whole
            wd[(2 * v + 1) * blocks : (2 * v + 2) * blocks, :] = whole

    def stacked(values):
        return jnp.concatenate([jnp.concatenate(halves(x), axis=1) for x in values], axis=0)

    span = group * tiles * blocks
    groups = devices // group
    total_rows = devices * tiles * blocks
    members = [(m, k) for m in range(group) for k in range(tiles)]
    def mix(g, w, slot):
        for i, (m, k) in enumerate(members):
            total = None
            for v in range(views):
                here = f[pl.ds(g * span + v * total_rows + i * blocks, blocks), :]
                row = ((g * group + m) * per_device + v * tiles + k) * table_rows + w
                factor = coef[pl.ds(row, 8, stride=0), :]
                term = jnp.concatenate([factor] * (blocks // 8), axis=0) * here
                total = term if total is None else total + term
            high, low = halves(total)
            rows = slice(i * blocks, (i + 1) * blocks)
            slot[rows, :LANES] = high
            slot[rows, LANES:] = low

    def gather(g, w, slot, hd):
        h = jnp.dot(slot[...], resp[w], preferred_element_type=jnp.float32)
        for i in range(len(members)):
            part = h[i * blocks : (i + 1) * blocks, :]
            hd[2 * i * blocks : (2 * i + 1) * blocks, :] = part
            hd[(2 * i + 1) * blocks : (2 * i + 2) * blocks, :] = part
        total = gy[w * blocks : (w + 1) * blocks, :]
        for i, (m, k) in enumerate(members):
            total = total + turn(hd, 2 * i * blocks, g * group + m, w * tiles + k, -1)
        gy[w * blocks : (w + 1) * blocks, :] = total

    def apply():
        def spread_views(g, count):
            for v in range(views):
                lhs = stacked(
                    [
                        turn(wd, 2 * v * blocks, g * count + n, v * tiles + k, 1)
                        for n in range(count)
                        for k in range(tiles)
                    ]
                )
                at = v * total_rows + g * (count * tiles * blocks)
                f[pl.ds(at, count * tiles * blocks), :] = jnp.dot(
                    lhs, resp_t[v], preferred_element_type=jnp.float32
                )

        if groups <= 2:
            spread_views(0, devices)
        else:
            lax.fori_loop(0, groups, lambda g, carry: (spread_views(g, group), carry)[1], 0)
        gy[...] = jnp.zeros_like(gy)

        def one(g):
            for w in range(0, views, 2):
                slots = [z2.at[(w + n) % 4] for n in range(2)]
                for n in range(2):
                    mix(g, w + n, slots[n])
                for n in range(2):
                    gather(g, w + n, slots[n], hds[(w + n) % 4])

        if groups <= 2:
            for g in range(groups):
                one(g)
        else:
            lax.fori_loop(0, groups, lambda g, carry: (one(g), carry)[1], 0)

    start = meas[...] - (first[:size, :] + second[:size, :])
    y[...] = start
    double(start)
    zero = jnp.zeros_like(start)
    d[...] = zero
    gd[...] = zero
    step[...] = zero

    def broadcast_tables(n, src):
        def one(device, carry):
            here = src[pl.ds(pl.multiple_of(size + device * table_rows, 8), table_rows), :]
            at = (n * half + device) * per_device
            for c in range(per_device):
                rows = pl.ds(pl.multiple_of((at + c) * table_rows, 8), table_rows)
                coef[rows, :] = jnp.broadcast_to(here[:, c : c + 1], here.shape)
            return carry

        lax.fori_loop(0, half, one, 0)

    broadcast_tables(0, first)
    broadcast_tables(1, second)
    to_scalars.wait()

    def iterate(n, norm_before):
        apply()
        new_y, new_gy = y[...], gy[...]
        norm = jnp.sum(new_y * new_gy)
        beta = jnp.where(n == 0, 0.0, norm / norm_before)
        new_d = new_y + beta * d[...]
        new_gd = new_gy + beta * gd[...]
        product = jnp.sum(new_gd * new_gd) + jnp.sum(new_d * new_gd) / TAU_STEP
        alpha = norm / product
        d[...] = new_d
        gd[...] = new_gd
        step[...] = step[...] + alpha * new_d
        new_y = new_y - alpha * (new_gd + new_d / TAU_STEP)
        y[...] = new_y
        double(new_y)
        return norm

    lax.fori_loop(0, CG_ITERS, iterate, jnp.float32(1.0))

    double(step[...])
    own = tiles * blocks
    for v in range(views):
        lhs = stacked(
            [
                pull(
                    lambda q: wd[pl.ds(2 * v * blocks + q, blocks), :],
                    bins[k, angles[0, v]], lane,
                )
                for k in range(tiles)
            ]
        )
        fs[v * own : (v + 1) * own, :] = jnp.dot(
            lhs, resp_t[v], preferred_element_type=jnp.float32
        )
    for b in range(0, blocks, 2):
        picked = [fs[pl.ds(b + n, views * tiles, stride=blocks), :] for n in range(2)]
        here = slice(b * LANES, (b + 2) * LANES)
        out[:, here] = (
            image[:, here]
            - TAU_STEP * (behind[:, here] - dual_new[:, here])
            + product(spread[...], jnp.concatenate(picked, axis=1))
        )


VMEM = pl.BlockSpec(memory_space=pltpu.VMEM)
SMEM = pl.BlockSpec(memory_space=pltpu.SMEM)


def f32(*shape):
    return pltpu.VMEM(shape, jnp.float32)


def kernel(body, name, out_shape, scalars, arrays, scratch=(), limit=16 << 20):
    single = not isinstance(out_shape, tuple)
    return pl.pallas_call(
        body,
        out_shape=out_shape,
        in_specs=[SMEM] * len(scalars) + [VMEM] * len(arrays),
        out_specs=VMEM if single else (VMEM,) * len(out_shape),
        scratch_shapes=list(scratch),
        compiler_params=pltpu.CompilerParams(vmem_limit_bytes=limit),
        name=name,
    )(
        *scalars,
        *(pltpu.with_memory_space_constraint(a, pltpu.MemorySpace.VMEM) for a in arrays),
    )


def exchange(x, sizes, ahead, mask):
    phases, rows = sizes
    pairs = [
        (t * rows + r, ((t + ahead) % phases) * rows + (r ^ mask))
        for t in range(phases)
        for r in range(rows)
    ]
    return lax.ppermute(x, ("tm", "row"), pairs)


def local(image, relaxed, dual, sinogram, angle_index, bin_offset, row_weight, response, row_gain):
    phases, devices = lax.axis_size("tm"), lax.axis_size("row")
    sizes = (phases, devices)
    num_rows, cols = image.shape[2:]
    views = angle_index.shape[1]
    tiles = bin_offset.shape[0]
    blocks = cols // LANES
    size = views * blocks
    image2, relaxed2, dual2 = (a.reshape(num_rows, cols) for a in (image, relaxed, dual))

    ring = [(i, (i - 1) % phases) for i in range(phases)]
    next_angles = lax.ppermute(angle_index, "tm", ring)
    ahead = lax.ppermute(relaxed2, "tm", ring)

    gain = row_gain.reshape(1, num_rows)
    meas = sinogram.reshape(size, LANES)
    table_rows = -(-(views + 1) // 8) * 8
    dims = dict(tiles=tiles, views=views, blocks=blocks)
    twice = pltpu.VMEM((views, 2 * LANES, LANES), jnp.bfloat16)
    spreads = f32(views * tiles, num_rows)
    tall = pltpu.VMEM((row_weight.shape[0], num_rows), jnp.float32)

    resp, resp_t, spread, spread_t, table, before = kernel(
        functools.partial(own_kernel, **dims),
        "own_tables",
        (
            twice, twice, spreads, f32(num_rows, views * tiles), f32(table_rows, LANES),
            f32(size, LANES),
        ),
        (angle_index, bin_offset),
        (image2, row_weight, gain, response),
        project_scratch(1, **dims) + [pltpu.VMEM((table_rows, num_rows), jnp.float32), tall],
    )
    resp_next, spread_next = kernel(
        functools.partial(next_kernel, tiles=tiles, views=views),
        "next_tables",
        (twice, spreads),
        (next_angles,),
        (row_weight, gain, response),
        [tall],
    )
    dual_new, msg, msg_next = kernel(
        functools.partial(dual_kernel, **dims),
        "dual_project",
        (f32(num_rows, cols), f32(size + table_rows, LANES), f32(size, LANES)),
        (angle_index, next_angles, bin_offset),
        (dual2, relaxed2, ahead, spread, spread_next, resp, resp_next, before, table),
        project_scratch(2, **dims),
    )

    masks = [1 << b if b < 2 else 3 << (b - 1) for b in range(devices.bit_length() - 1)]
    got = exchange(msg, sizes, 0, masks[0])
    got_next = exchange(msg_next, sizes, 1, 0)
    got_cross = exchange(msg_next, sizes, 1, masks[0])
    total = msg[:size] + got[:size] + (got_next + got_cross)
    tables = jnp.concatenate([msg[size:], got[size:]], axis=0)
    for mask in masks[1:]:
        msg = jnp.concatenate([total, tables], axis=0)
        got = exchange(msg, sizes, 0, mask)
        total = msg[:size] + got[:size]
        tables = jnp.concatenate([msg[size:], got[size:]], axis=0)
    behind = lax.ppermute(dual_new, "tm", [(i, (i + 1) % phases) for i in range(phases)])

    group = max(1, 16 // tiles)
    while devices % group:
        group //= 2
    whole = devices * tiles * blocks
    image_new = kernel(
        functools.partial(
            cg_kernel, **dims, devices=devices, group=group, table_rows=table_rows
        ),
        "sinogram_cg",
        jax.ShapeDtypeStruct((num_rows, cols), jnp.float32),
        (angle_index, bin_offset),
        (msg, got, meas, resp, resp_t, spread_t, image2, dual_new, behind),
        [pltpu.VMEM((size, LANES), jnp.float32)] * 5
        + [
            pltpu.VMEM((2 * size, LANES), jnp.float32),
            pltpu.VMEM((views * whole, LANES), jnp.float32),
            pltpu.VMEM((4, group * tiles * blocks, 2 * LANES), jnp.bfloat16),
        ]
        + [pltpu.VMEM((2 * group * tiles * blocks, LANES), jnp.float32)] * 4
        + [
            pltpu.VMEM((views * tiles * blocks, LANES), jnp.float32),
            pltpu.VMEM((devices * tiles * views * table_rows, LANES), jnp.float32),
            pltpu.VMEM((4 * devices, LANES), jnp.int32),
            pltpu.SMEM((4 * devices, LANES), jnp.int32),
            pltpu.SemaphoreType.DMA,
        ],
        limit=(12 << 20) + 8 * views * whole * LANES,
    )
    return image_new.reshape(image.shape), dual_new.reshape(dual.shape)


def solution(mesh):
    return jax.shard_map(
        local,
        mesh=mesh,
        in_specs=(
            P("tm", None, "row", None),
            P("tm", None, "row", None),
            P("tm", None, "row", None),
            P("tm", None, None, None),
            P("tm", None),
            P("row", None),
            P(),
            P(),
            P("row"),
        ),
        out_specs=(P("tm", None, "row", None), P("tm", None, "row", None)),
        check_vma=False,
    )
```

```python
import functools

import jax
import jax.numpy as jnp
from jax import lax
from jax.experimental import pallas as pl
from jax.experimental.pallas import tpu as pltpu
from jax.sharding import PartitionSpec as P


CG_ITERS = 3
TAU_STEP = 0.1
SIGMA_STEP = 2.0
LAMBDA_BOUND = 2.0
HIGH = lax.Precision.HIGHEST
LANES = 128


def halves(x):
    high = x.astype(jnp.bfloat16)
    low = (x - high.astype(jnp.float32)).astype(jnp.bfloat16)
    return high, low


def product(a, b):
    (ah, al), (bh, bl) = halves(a), halves(b)
    dot = functools.partial(jnp.dot, preferred_element_type=jnp.float32)
    return dot(ah, bh) + (dot(ah, bl) + dot(al, bh))


def lane_index(rows):
    return lax.broadcasted_iota(jnp.int32, (rows, LANES), 1)


def pull(load, offset, lane):
    block, rest = offset >> 7, offset & (LANES - 1)
    mixed = jnp.where(lane < rest, load(block + 1), load(block))
    return pltpu.roll(mixed, (LANES - rest) & (LANES - 1), 1)


def push(load, offset, lane, blocks):
    block, rest = offset >> 7, offset & (LANES - 1)
    mixed = jnp.where(lane >= LANES - rest, load(blocks - 1 - block), load(blocks - block))
    return pltpu.roll(mixed, rest, 1)


def project_sets(stack, bins, tables, zs, hd, tiles, views, blocks):
    lane = lane_index(blocks)
    rows = tiles * blocks
    total = stack.shape[0]
    for b in range(blocks):
        zs[pl.ds(b, total, stride=blocks), :] = stack[:, b * LANES : (b + 1) * LANES]
    for s, (response, angles, out, init) in enumerate(tables):
        for v in range(views):
            at = (s * views + v) * rows
            lhs = jnp.concatenate(halves(zs[at : at + rows, :]), axis=1)
            h = jnp.dot(lhs, response[v], preferred_element_type=jnp.float32)
            for k in range(tiles):
                part = h[k * blocks : (k + 1) * blocks, :]
                hd[2 * at + 2 * k * blocks : 2 * at + (2 * k + 1) * blocks, :] = part
                hd[2 * at + (2 * k + 1) * blocks : 2 * at + (2 * k + 2) * blocks, :] = part
            whole = None if init is None else init[v * blocks : (v + 1) * blocks, :]
            for k in range(tiles):
                part = push(
                    lambda q: hd[pl.ds(2 * at + 2 * k * blocks + q, blocks), :],
                    bins[k, angles[0, v]], lane, blocks,
                )
                whole = part if whole is None else whole + part
            out[v * blocks : (v + 1) * blocks, :] = whole


def project_scratch(sets, tiles, views, blocks):
    rows = sets * views * tiles * blocks
    return [pltpu.VMEM((rows, LANES), jnp.float32), pltpu.VMEM((2 * rows, LANES), jnp.float32)]


def fetch_responses(angles, response, resp, sems, views):
    copies = [
        pltpu.make_async_copy(
            response.at[angles[0, v]], resp.at[v, n * LANES : (n + 1) * LANES, :],
            sems.at[2 * v + n],
        )
        for v in range(views)
        for n in range(2)
    ]
    for copy in copies:
        copy.start()
    return copies


def view_weights(angles, gained, spread, tiles, views):
    width = gained.shape[1]
    row = lax.broadcasted_iota(jnp.int32, (tiles, width), 0)
    column = lax.broadcasted_iota(jnp.int32, (tiles, width), 1) // (width // tiles)
    for v in range(views):
        line = jnp.broadcast_to(gained[pl.ds(angles[0, v], 1), :], (tiles, width))
        spread[v * tiles : (v + 1) * tiles, :] = jnp.where(row == column, line, 0.0)


def own_kernel(
    angles, bins, weights, gain, image, dual, relaxed, response,
    resp, resp_t, spread, spread_t, table, before, rest, gained, zs, hd, chosen, table_w, table_g,
    planes, sems,
    *, tiles, views, blocks,
):
    copies = fetch_responses(angles, response, resp, sems, views)
    for n, source in enumerate((image, dual, relaxed)):
        copies.append(pltpu.make_async_copy(source, planes.at[n], sems.at[2 * views + n]))
        copies[-1].start()
    small = [
        pltpu.make_async_copy(source, target, sems.at[2 * views + 3 + n])
        for n, (source, target) in enumerate(((weights, table_w), (gain, table_g)))
    ]
    for copy in small:
        copy.start()
    for copy in small:
        copy.wait()
    width = table_w.shape[0]
    for k in range(tiles):
        gained[:, k * width : (k + 1) * width] = table_w[...].T
    gained[...] = gained[...] * table_g[...]
    view_weights(angles, gained, spread, tiles, views)
    mine = spread[...]
    spread_t[...] = mine.T
    chosen[...] = jnp.zeros_like(chosen)
    for v in range(views):
        chosen[v : v + 1, :] = gained[pl.ds(angles[0, v], 1), :]
    coupling = lax.dot_general(
        chosen[...], mine, (((1,), (1,)), ((), ())),
        precision=HIGH, preferred_element_type=jnp.float32,
    )
    table[...] = jnp.zeros_like(table)
    half = views // 2
    table[:half, : views * tiles] = coupling[:half, :]
    table[:half, LANES // 2 : LANES // 2 + views * tiles] = coupling[half:views, :]
    lane = lane_index(8)
    offsets = jnp.zeros((8, LANES), jnp.int32)
    for v in range(views):
        for k in range(tiles):
            offsets = jnp.where(lane == v * tiles + k, bins[k, angles[0, v]], offsets)
    table[half : half + 1, :] = offsets[:1, :].astype(jnp.float32)
    for copy in copies[: 2 * views + 1]:
        copy.wait()
    for v in range(views):
        turned = resp[v, :LANES, :].astype(jnp.float32).T.astype(jnp.bfloat16)
        resp_t[v, :LANES, :] = turned
        resp_t[v, LANES:, :] = turned
    project_sets(
        product(mine, planes[0]), bins, [(resp, angles, before, None)],
        zs, hd, tiles, views, blocks,
    )
    for copy in copies[2 * views + 1 :]:
        copy.wait()
    rest[...] = planes[1] - SIGMA_STEP * planes[2]


def next_kernel(angles, gained, response, resp, spread, sems, *, tiles, views):
    copies = fetch_responses(angles, response, resp, sems, views)
    view_weights(angles, gained, spread, tiles, views)
    for copy in copies:
        copy.wait()


def dual_kernel(
    angles, angles_next, bins, rest, ahead, spread, spread_next, resp, resp_next,
    before, table, dual_new, msg_own, msg_next, zs, hd, *, tiles, views, blocks,
):
    fresh = jnp.clip(rest[...] + SIGMA_STEP * ahead[...], -LAMBDA_BOUND, LAMBDA_BOUND)
    dual_new[...] = fresh
    both = jnp.concatenate([TAU_STEP * spread[...], -TAU_STEP * spread_next[...]], axis=0)
    project_sets(
        product(both, fresh), bins,
        [(resp, angles, msg_own, before), (resp_next, angles_next, msg_next, None)],
        zs, hd, tiles, views, blocks,
    )
    msg_own[views * blocks :, :] = table[...]


def couple_kernel(first, out, xs, *, size, tiles, views, blocks, table_rows):
    here = jnp.concatenate(halves(first[size:, :]), axis=0)
    count = here.shape[0]
    half_views = views // 2
    row = lax.broadcasted_iota(jnp.int32, (LANES, 2 * LANES), 0)
    column = lax.broadcasted_iota(jnp.int32, (LANES, 2 * LANES), 1)
    for k in range(tiles):
        for side in range(2):
            source = side * (LANES // 2) + (column // blocks) * tiles + k
            pick = jnp.where((row == source) & (column < views * blocks), 1.0, 0.0)
            at = (k * 2 + side) * count
            xs[at : at + count, :] = jnp.dot(
                here, pick.astype(jnp.bfloat16), preferred_element_type=jnp.float32
            )
    diagonal = (
        lax.broadcasted_iota(jnp.int32, (blocks, 2 * LANES), 1) % blocks
        == lax.broadcasted_iota(jnp.int32, (blocks, 2 * LANES), 0)
    )

    def one(device, carry):
        for k in range(tiles):
            for w in range(views):
                for piece in range(2):
                    at = (k * 2 + w // half_views) * count + piece * (count // 2) + w % half_views
                    line = xs[pl.ds(at + device * table_rows, 1), :]
                    block = jnp.where(diagonal, jnp.broadcast_to(line, diagonal.shape), 0.0)
                    rows = slice(w * blocks, (w + 1) * blocks)
                    out[device * tiles + k, piece, rows, :] = block.astype(jnp.bfloat16)
        return carry

    lax.fori_loop(0, count // (2 * table_rows), one, 0)


def cg_kernel(
    angles, bins, couple, first, second, meas, resp, resp_t, spread, image, dual_new, behind,
    out, y, d, gd, gy, step, wd, f, right, z2, zs, hd0, hd1, hd2, hd3, fs, coef, shifts_v, shifts,
    sem,
    *, tiles, views, blocks, devices, group, table_rows,
):
    hds = (hd0, hd1, hd2, hd3)
    lane = lane_index(blocks)
    size = views * blocks
    half = devices // 2
    per_device = tiles * views
    half_views = views // 2
    for n, src in enumerate((first, second)):
        there = src[pl.ds(size + half_views, half, stride=table_rows), :].astype(jnp.int32)
        back = (blocks * LANES - there) & (blocks * LANES - 1)
        for m, value in enumerate((there >> 7, there & (LANES - 1), back >> 7, back & (LANES - 1))):
            shifts_v[m * devices + n * half : m * devices + (n + 1) * half, :] = value
    to_scalars = pltpu.make_async_copy(shifts_v, shifts, sem)
    to_scalars.start()

    def turn(src, base, device, at, sign):
        mine, other = (0, 2 * devices) if sign > 0 else (2 * devices, 0)
        block = shifts[mine + device, at]
        rest = shifts[mine + devices + device, at]
        back = shifts[other + devices + device, at]
        row = base + block
        mixed = jnp.where(
            lane < rest, src[pl.ds(row + 1, blocks), :], src[pl.ds(row, blocks), :]
        )
        return pltpu.roll(mixed, back, 1)

    def double(src):
        for v in range(views):
            whole = src[v * blocks : (v + 1) * blocks, :]
            wd[2 * v * blocks : (2 * v + 1) * blocks, :] = whole
            wd[(2 * v + 1) * blocks : (2 * v + 2) * blocks, :] = whole

    def stacked(values):
        return jnp.concatenate([jnp.concatenate(halves(x), axis=1) for x in values], axis=0)

    span = group * tiles * blocks
    groups = half // group
    half_rows = half * tiles * blocks
    members = [(m, k) for m in range(group) for k in range(tiles)]

    def turned(n, g, v):
        return [
            turn(wd, 2 * v * blocks, n * half + g * group + m, v * tiles + k, 1)
            for m, k in members
        ]

    def keep_first(g, v, h):
        high, low = halves(h)
        for i, (m, k) in enumerate(members):
            rows = slice(i * blocks, (i + 1) * blocks)
            to = slice(v * blocks, (v + 1) * blocks)
            right[g * len(members) + i, to, :LANES] = high[rows, :]
            right[g * len(members) + i, to, LANES:] = low[rows, :]

    def keep_second(g, v, h):
        f[pl.ds(v * half_rows + g * span, span), :] = h

    def spread_views(g):
        for v in range(views):
            lhs = stacked(turned(0, g, v) + turned(1, g, v))
            h = jnp.dot(lhs, resp_t[v], preferred_element_type=jnp.float32)
            keep_first(g, v, h[:span, :])
            keep_second(g, v, h[span:, :])

    def mix_first(g):
        for i in range(len(members)):
            t = g * len(members) + i
            both = jnp.dot(couple[t, 0], right[t], preferred_element_type=jnp.float32)
            both = both + jnp.dot(couple[t, 1], right[t], preferred_element_type=jnp.float32)
            mixed = both[:, :LANES] + both[:, LANES:]
            high, low = halves(mixed)
            for w in range(views):
                rows = slice(w * blocks, (w + 1) * blocks)
                zs[w, i * blocks : (i + 1) * blocks, :LANES] = high[rows, :]
                zs[w, i * blocks : (i + 1) * blocks, LANES:] = low[rows, :]

    def mix_second(g, w, slot):
        for i, (m, k) in enumerate(members):
            total = None
            for v in range(views):
                here = f[pl.ds(g * span + v * half_rows + i * blocks, blocks), :]
                row = (g * group + m) * per_device + v * tiles + k
                row = (2 * row + w // half_views) * table_rows + w % half_views
                factor = coef[pl.ds(row, 8, stride=0), :]
                term = jnp.concatenate([factor] * (blocks // 8), axis=0) * here
                total = term if total is None else total + term
            high, low = halves(total)
            rows = slice(i * blocks, (i + 1) * blocks)
            slot[rows, :LANES] = high
            slot[rows, LANES:] = low

    def gather(n, g, w, slot, hd):
        h = jnp.dot(slot[...], resp[w], preferred_element_type=jnp.float32)
        for i in range(len(members)):
            part = h[i * blocks : (i + 1) * blocks, :]
            hd[2 * i * blocks : (2 * i + 1) * blocks, :] = part
            hd[(2 * i + 1) * blocks : (2 * i + 2) * blocks, :] = part
        total = gy[w * blocks : (w + 1) * blocks, :]
        for i, (m, k) in enumerate(members):
            device = n * half + g * group + m
            total = total + turn(hd, 2 * i * blocks, device, w * tiles + k, -1)
        gy[w * blocks : (w + 1) * blocks, :] = total

    def mix_and_gather(g):
        mix_first(g)
        for w in range(views):
            mix_second(g, w, z2.at[w % 4])
            gather(1, g, w, z2.at[w % 4], hds[w % 2])
            gather(0, g, w, zs.at[w], hds[2 + w % 2])

    def apply():
        gy[...] = jnp.zeros_like(gy)
        if groups == 1:
            spread_views(0)
            mix_and_gather(0)
        else:
            lax.fori_loop(0, groups, lambda g, carry: (spread_views(g), carry)[1], 0)
            lax.fori_loop(0, groups, lambda g, carry: (mix_and_gather(g), carry)[1], 0)

    start = meas[...] - (first[:size, :] + second[:size, :])
    y[...] = start
    double(start)
    zero = jnp.zeros_like(start)
    d[...] = zero
    gd[...] = zero
    step[...] = zero
    for t in range(half * tiles):
        right[t, size:, :] = jnp.zeros((2 * LANES - size, 2 * LANES), jnp.bfloat16)

    def broadcast_one(device, carry):
        here = second[pl.ds(pl.multiple_of(size + device * table_rows, 8), table_rows), :]
        for c in range(per_device):
            for side in range(2):
                rows = pl.multiple_of((2 * (device * per_device + c) + side) * table_rows, 8)
                lane_of = side * (LANES // 2) + c
                coef[pl.ds(rows, table_rows), :] = jnp.broadcast_to(
                    here[:, lane_of : lane_of + 1], here.shape
                )
        return carry

    lax.fori_loop(0, half, broadcast_one, 0)
    to_scalars.wait()

    def iterate(n, norm_before):
        apply()
        new_y, new_gy = y[...], gy[...]
        norm = jnp.sum(new_y * new_gy)
        beta = jnp.where(n == 0, 0.0, norm / norm_before)
        new_d = new_y + beta * d[...]
        new_gd = new_gy + beta * gd[...]
        product = jnp.sum(new_gd * new_gd) + jnp.sum(new_d * new_gd) / TAU_STEP
        alpha = norm / product
        d[...] = new_d
        gd[...] = new_gd
        step[...] = step[...] + alpha * new_d
        new_y = new_y - alpha * (new_gd + new_d / TAU_STEP)
        y[...] = new_y
        double(new_y)
        return norm

    lax.fori_loop(0, CG_ITERS, iterate, jnp.float32(1.0))

    double(step[...])
    own = tiles * blocks
    for v in range(views):
        lhs = stacked(
            [
                pull(
                    lambda q: wd[pl.ds(2 * v * blocks + q, blocks), :],
                    bins[k, angles[0, v]], lane,
                )
                for k in range(tiles)
            ]
        )
        fs[v * own : (v + 1) * own, :] = jnp.dot(
            lhs, resp_t[v], preferred_element_type=jnp.float32
        )
    for b in range(0, blocks, 2):
        picked = [fs[pl.ds(b + n, views * tiles, stride=blocks), :] for n in range(2)]
        here = slice(b * LANES, (b + 2) * LANES)
        out[:, here] = (
            image[:, here]
            - TAU_STEP * (behind[:, here] - dual_new[:, here])
            + product(spread[...], jnp.concatenate(picked, axis=1))
        )


VMEM = pl.BlockSpec(memory_space=pltpu.VMEM)
SMEM = pl.BlockSpec(memory_space=pltpu.SMEM)
PLACE = pl.BlockSpec(memory_space=pl.ANY)


def f32(*shape):
    return pltpu.VMEM(shape, jnp.float32)


def stay(x):
    return pltpu.with_memory_space_constraint(x, pltpu.MemorySpace.HBM)


def kernel(body, out_shape, scalars, arrays, scratch=(), limit=16 << 20, in_place=()):
    single = not isinstance(out_shape, tuple)
    return pl.pallas_call(
        body,
        out_shape=out_shape,
        in_specs=[SMEM] * len(scalars) + [VMEM] * len(arrays) + [PLACE] * len(in_place),
        out_specs=VMEM if single else (VMEM,) * len(out_shape),
        scratch_shapes=list(scratch),
        compiler_params=pltpu.CompilerParams(vmem_limit_bytes=limit),
    )(
        *(stay(a) if lies else a for a, lies in scalars),
        *(pltpu.with_memory_space_constraint(a, pltpu.MemorySpace.VMEM) for a in arrays),
        *map(stay, in_place),
    )


def exchange(x, sizes, ahead, mask):
    phases, rows = sizes
    pairs = [
        (t * rows + r, ((t + ahead) % phases) * rows + (r ^ mask))
        for t in range(phases)
        for r in range(rows)
    ]
    return lax.ppermute(x, ("tm", "row"), pairs)


def local(image, relaxed, dual, sinogram, angle_index, bin_offset, row_weight, response, row_gain):
    phases, devices = lax.axis_size("tm"), lax.axis_size("row")
    sizes = (phases, devices)
    num_rows, cols = image.shape[2:]
    views = angle_index.shape[1]
    tiles = bin_offset.shape[0]
    blocks = cols // LANES
    size = views * blocks
    image2, relaxed2, dual2 = (a.reshape(num_rows, cols) for a in (image, relaxed, dual))

    ring = [(i, (i - 1) % phases) for i in range(phases)]
    next_angles = lax.ppermute(angle_index, "tm", ring)
    ahead = lax.ppermute(relaxed2, "tm", ring)

    gain = row_gain.reshape(1, num_rows)
    meas = sinogram.reshape(size, LANES)
    table_rows = -(-(views // 2 + 1) // 8) * 8
    assert views % 2 == 0 and tiles * views <= LANES // 2
    dims = dict(tiles=tiles, views=views, blocks=blocks)
    twice = pltpu.VMEM((views, 2 * LANES, LANES), jnp.bfloat16)
    spreads = f32(views * tiles, num_rows)
    tall = pltpu.VMEM((row_weight.shape[0], num_rows), jnp.float32)

    own_angles, offsets = (angle_index, True), (bin_offset, True)
    resp, resp_t, spread, spread_t, table, before, rest, gained = kernel(
        functools.partial(own_kernel, **dims),
        (
            twice, twice, spreads, f32(num_rows, views * tiles), f32(table_rows, LANES),
            f32(size, LANES), f32(num_rows, cols), tall,
        ),
        (own_angles, offsets),
        (),
        project_scratch(1, **dims)
        + [
            pltpu.VMEM((-(-views // 8) * 8, num_rows), jnp.float32),
            pltpu.VMEM(row_weight.shape[::-1], jnp.float32),
            pltpu.VMEM(gain.shape, jnp.float32),
            pltpu.VMEM((3, num_rows, cols), jnp.float32),
            pltpu.SemaphoreType.DMA((2 * views + 5,)),
        ],
        in_place=(row_weight.T, gain, image2, dual2, relaxed2, response),
    )
    resp_next, spread_next = kernel(
        functools.partial(next_kernel, tiles=tiles, views=views),
        (twice, spreads),
        ((next_angles, False),),
        (gained,),
        [pltpu.SemaphoreType.DMA((2 * views,))],
        in_place=(response,),
    )
    dual_new, msg, msg_next = kernel(
        functools.partial(dual_kernel, **dims),
        (f32(num_rows, cols), f32(size + table_rows, LANES), f32(size, LANES)),
        (own_angles, (next_angles, False), offsets),
        (rest, ahead, spread, spread_next, resp, resp_next, before, table),
        project_scratch(2, **dims),
    )

    masks = [1 << b if b < 2 else 3 << (b - 1) for b in range(devices.bit_length() - 1)]
    masks = masks[:1] + masks[:0:-1]
    got = exchange(msg, sizes, 0, masks[0])
    got_next = exchange(msg_next, sizes, 1, 0)
    got_cross = exchange(msg_next, sizes, 1, masks[0])
    total = msg[:size] + got[:size] + (got_next + got_cross)
    tables = jnp.concatenate([msg[size:], got[size:]], axis=0)
    for mask in masks[1:]:
        msg = jnp.concatenate([total, tables], axis=0)
        got = exchange(msg, sizes, 0, mask)
        total = msg[:size] + got[:size]
        tables = jnp.concatenate([msg[size:], got[size:]], axis=0)
    half = devices // 2
    couple = kernel(
        functools.partial(couple_kernel, size=size, table_rows=table_rows, **dims),
        pltpu.VMEM((half * tiles, 2, size, 2 * LANES), jnp.bfloat16),
        (),
        (msg,),
        [pltpu.VMEM((4 * half * tiles * table_rows, 2 * LANES), jnp.float32)],
        limit=(4 << 20) + half * tiles * (4 * table_rows * 2 * LANES * 4),
    )
    behind = lax.ppermute(dual_new, "tm", [(i, (i + 1) % phases) for i in range(phases)])

    group = max(1, 16 // tiles)
    while half % group:
        group //= 2
    whole = half * tiles * blocks
    span = group * tiles * blocks
    image_new = kernel(
        functools.partial(
            cg_kernel, **dims, devices=devices, group=group, table_rows=table_rows
        ),
        jax.ShapeDtypeStruct((num_rows, cols), jnp.float32),
        (own_angles, offsets),
        (couple, msg, got, meas, resp, resp_t, spread_t, image2, dual_new, behind),
        [pltpu.VMEM((size, LANES), jnp.float32)] * 5
        + [
            pltpu.VMEM((2 * size, LANES), jnp.float32),
            pltpu.VMEM((views * whole, LANES), jnp.float32),
            pltpu.VMEM((half * tiles, 2 * LANES, 2 * LANES), jnp.bfloat16),
            pltpu.VMEM((4, span, 2 * LANES), jnp.bfloat16),
            pltpu.VMEM((views, span, 2 * LANES), jnp.bfloat16),
        ]
        + [pltpu.VMEM((2 * span, LANES), jnp.float32)] * 4
        + [
            pltpu.VMEM((views * tiles * blocks, LANES), jnp.float32),
            pltpu.VMEM((2 * half * tiles * views * table_rows, LANES), jnp.float32),
            pltpu.VMEM((4 * devices, LANES), jnp.int32),
            pltpu.SMEM((4 * devices, LANES), jnp.int32),
            pltpu.SemaphoreType.DMA,
        ],
        limit=(12 << 20) + 14 * views * whole * LANES,
    )
    return image_new.reshape(image.shape), dual_new.reshape(dual.shape)


def solution(mesh):
    return jax.shard_map(
        local,
        mesh=mesh,
        in_specs=(
            P("tm", None, "row", None),
            P("tm", None, "row", None),
            P("tm", None, "row", None),
            P("tm", None, None, None),
            P("tm", None),
            P("row", None),
            P(),
            P(),
            P("row"),
        ),
        out_specs=(P("tm", None, "row", None), P("tm", None, "row", None)),
        check_vma=False,
    )
```

```python
import functools

import jax
import jax.numpy as jnp
from jax import lax
from jax.experimental import pallas as pl
from jax.experimental.pallas import tpu as pltpu
from jax.sharding import PartitionSpec as P


CG_ITERS = 3
TAU_STEP = 0.1
SIGMA_STEP = 2.0
LAMBDA_BOUND = 2.0
HIGH = lax.Precision.HIGHEST
LANES = 128


def halves(x):
    high = x.astype(jnp.bfloat16)
    low = (x - high.astype(jnp.float32)).astype(jnp.bfloat16)
    return high, low


def product(a, b):
    (ah, al), (bh, bl) = halves(a), halves(b)
    rows = a.shape[0]
    dot = functools.partial(jnp.dot, preferred_element_type=jnp.float32)
    both = dot(jnp.concatenate([ah, al], axis=0), bh)
    return both[:rows] + (both[rows:] + dot(ah, bl))


def lane_index(rows):
    return lax.broadcasted_iota(jnp.int32, (rows, LANES), 1)


def pull(load, offset, lane):
    block, rest = offset >> 7, offset & (LANES - 1)
    mixed = jnp.where(lane < rest, load(block + 1), load(block))
    return pltpu.roll(mixed, (LANES - rest) & (LANES - 1), 1)


def push(load, offset, lane, blocks):
    block, rest = offset >> 7, offset & (LANES - 1)
    mixed = jnp.where(lane >= LANES - rest, load(blocks - 1 - block), load(blocks - block))
    return pltpu.roll(mixed, rest, 1)


def project_sets(stack, bins, tables, zs, hd, tiles, views, blocks):
    lane = lane_index(blocks)
    rows = tiles * blocks
    total = stack.shape[0]
    for b in range(blocks):
        zs[pl.ds(b, total, stride=blocks), :] = stack[:, b * LANES : (b + 1) * LANES]
    for s, (response, angles, out, init) in enumerate(tables):
        for v in range(views):
            at = (s * views + v) * rows
            lhs = jnp.concatenate(halves(zs[at : at + rows, :]), axis=1)
            h = jnp.dot(lhs, response[v], preferred_element_type=jnp.float32)
            for k in range(tiles):
                part = h[k * blocks : (k + 1) * blocks, :]
                hd[2 * at + 2 * k * blocks : 2 * at + (2 * k + 1) * blocks, :] = part
                hd[2 * at + (2 * k + 1) * blocks : 2 * at + (2 * k + 2) * blocks, :] = part
            whole = None if init is None else init[v * blocks : (v + 1) * blocks, :]
            for k in range(tiles):
                part = push(
                    lambda q: hd[pl.ds(2 * at + 2 * k * blocks + q, blocks), :],
                    bins[k, angles[0, v]], lane, blocks,
                )
                whole = part if whole is None else whole + part
            out[v * blocks : (v + 1) * blocks, :] = whole


def project_scratch(sets, tiles, views, blocks):
    rows = sets * views * tiles * blocks
    return [pltpu.VMEM((rows, LANES), jnp.float32), pltpu.VMEM((2 * rows, LANES), jnp.float32)]


def fetch_responses(angles, response, resp, sems, views):
    copies = [
        pltpu.make_async_copy(
            response.at[angles[0, v]], resp.at[v, n * LANES : (n + 1) * LANES, :],
            sems.at[2 * v + n],
        )
        for v in range(views)
        for n in range(2)
    ]
    for copy in copies:
        copy.start()
    return copies


def view_weights(angles, gained, spread, tiles, views):
    width = gained.shape[1]
    row = lax.broadcasted_iota(jnp.int32, (tiles, width), 0)
    column = lax.broadcasted_iota(jnp.int32, (tiles, width), 1) // (width // tiles)
    for v in range(views):
        line = jnp.broadcast_to(gained[pl.ds(angles[0, v], 1), :], (tiles, width))
        spread[v * tiles : (v + 1) * tiles, :] = jnp.where(row == column, line, 0.0)


def own_kernel(
    angles, bins, weights, gain, image, dual, relaxed, response,
    resp, resp_t, spread, spread_t, table, before, rest, gained, zs, hd, chosen, table_w, table_g,
    planes, sems,
    *, tiles, views, blocks,
):
    copies = fetch_responses(angles, response, resp, sems, views)
    for n, source in enumerate((image, dual, relaxed)):
        copies.append(pltpu.make_async_copy(source, planes.at[n], sems.at[2 * views + n]))
        copies[-1].start()
    small = [
        pltpu.make_async_copy(source, target, sems.at[2 * views + 3 + n])
        for n, (source, target) in enumerate(((weights, table_w), (gain, table_g)))
    ]
    for copy in small:
        copy.start()
    for copy in small:
        copy.wait()
    width = table_w.shape[0]
    for k in range(tiles):
        gained[:, k * width : (k + 1) * width] = table_w[...].T
    gained[...] = gained[...] * table_g[...]
    view_weights(angles, gained, spread, tiles, views)
    mine = spread[...]
    spread_t[...] = mine.T
    chosen[...] = jnp.zeros_like(chosen)
    for v in range(views):
        chosen[v : v + 1, :] = gained[pl.ds(angles[0, v], 1), :]
    coupling = lax.dot_general(
        chosen[...], mine, (((1,), (1,)), ((), ())),
        precision=HIGH, preferred_element_type=jnp.float32,
    )
    table[...] = jnp.zeros_like(table)
    half = views // 2
    table[:half, : views * tiles] = coupling[:half, :]
    table[:half, LANES // 2 : LANES // 2 + views * tiles] = coupling[half:views, :]
    lane = lane_index(8)
    offsets = jnp.zeros((8, LANES), jnp.int32)
    for v in range(views):
        for k in range(tiles):
            offsets = jnp.where(lane == v * tiles + k, bins[k, angles[0, v]], offsets)
    table[half : half + 1, :] = offsets[:1, :].astype(jnp.float32)
    for copy in copies[: 2 * views + 1]:
        copy.wait()
    for v in range(views):
        turned = resp[v, :LANES, :].astype(jnp.float32).T.astype(jnp.bfloat16)
        resp_t[v, :LANES, :] = turned
        resp_t[v, LANES:, :] = turned
    project_sets(
        product(mine, planes[0]), bins, [(resp, angles, before, None)],
        zs, hd, tiles, views, blocks,
    )
    for copy in copies[2 * views + 1 :]:
        copy.wait()
    rest[...] = planes[1] - SIGMA_STEP * planes[2]


def next_kernel(angles, gained, response, resp, spread, sems, *, tiles, views):
    copies = fetch_responses(angles, response, resp, sems, views)
    view_weights(angles, gained, spread, tiles, views)
    for copy in copies:
        copy.wait()


def dual_kernel(
    angles, angles_next, bins, rest, ahead, spread, spread_next, resp, resp_next,
    before, table, dual_new, msg_own, msg_next, zs, hd, *, tiles, views, blocks,
):
    fresh = jnp.clip(rest[...] + SIGMA_STEP * ahead[...], -LAMBDA_BOUND, LAMBDA_BOUND)
    dual_new[...] = fresh
    both = jnp.concatenate([TAU_STEP * spread[...], -TAU_STEP * spread_next[...]], axis=0)
    project_sets(
        product(both, fresh), bins,
        [(resp, angles, msg_own, before), (resp_next, angles_next, msg_next, None)],
        zs, hd, tiles, views, blocks,
    )
    msg_own[views * blocks :, :] = table[...]


def couple_kernel(first, out, xs, *, size, tiles, views, blocks, table_rows):
    here = jnp.concatenate(halves(first[size:, :]), axis=0)
    count = here.shape[0]
    half_views = views // 2
    row = lax.broadcasted_iota(jnp.int32, (LANES, 2 * LANES), 0)
    column = lax.broadcasted_iota(jnp.int32, (LANES, 2 * LANES), 1)
    for k in range(tiles):
        for side in range(2):
            source = side * (LANES // 2) + (column // blocks) * tiles + k
            pick = jnp.where((row == source) & (column < views * blocks), 1.0, 0.0)
            at = (k * 2 + side) * count
            xs[at : at + count, :] = jnp.dot(
                here, pick.astype(jnp.bfloat16), preferred_element_type=jnp.float32
            )
    diagonal = (
        lax.broadcasted_iota(jnp.int32, (blocks, 2 * LANES), 1) % blocks
        == lax.broadcasted_iota(jnp.int32, (blocks, 2 * LANES), 0)
    )

    def one(device, carry):
        for k in range(tiles):
            for w in range(views):
                for piece in range(2):
                    at = (k * 2 + w // half_views) * count + piece * (count // 2) + w % half_views
                    line = xs[pl.ds(at + device * table_rows, 1), :]
                    block = jnp.where(diagonal, jnp.broadcast_to(line, diagonal.shape), 0.0)
                    rows = slice(w * blocks, (w + 1) * blocks)
                    out[device * tiles + k, piece, rows, :] = block.astype(jnp.bfloat16)
        return carry

    lax.fori_loop(0, count // (2 * table_rows), one, 0)


def cg_kernel(
    angles, bins, couple, first, second, meas, resp, resp_t, spread, image, dual_new, behind,
    out, y, d, gd, gy, step, wd, f, right, z2, zs, hd0, hd1, hd2, hd3, fs, coef, shifts_v, shifts,
    sem,
    *, tiles, views, blocks, devices, group, table_rows,
):
    hds = (hd0, hd1, hd2, hd3)
    lane = lane_index(blocks)
    size = views * blocks
    half = devices // 2
    per_device = tiles * views
    half_views = views // 2
    for n, src in enumerate((first, second)):
        there = src[pl.ds(size + half_views, half, stride=table_rows), :].astype(jnp.int32)
        back = (blocks * LANES - there) & (blocks * LANES - 1)
        for m, value in enumerate((there >> 7, there & (LANES - 1), back >> 7, back & (LANES - 1))):
            shifts_v[m * devices + n * half : m * devices + (n + 1) * half, :] = value
    to_scalars = pltpu.make_async_copy(shifts_v, shifts, sem)
    to_scalars.start()

    def turn(src, base, device, at, sign):
        mine, other = (0, 2 * devices) if sign > 0 else (2 * devices, 0)
        block = shifts[mine + device, at]
        rest = shifts[mine + devices + device, at]
        back = shifts[other + devices + device, at]
        row = base + block
        mixed = jnp.where(
            lane < rest, src[pl.ds(row + 1, blocks), :], src[pl.ds(row, blocks), :]
        )
        return pltpu.roll(mixed, back, 1)

    def double(src):
        for v in range(views):
            whole = src[v * blocks : (v + 1) * blocks, :]
            wd[2 * v * blocks : (2 * v + 1) * blocks, :] = whole
            wd[(2 * v + 1) * blocks : (2 * v + 2) * blocks, :] = whole

    def stacked(values):
        return jnp.concatenate([jnp.concatenate(halves(x), axis=1) for x in values], axis=0)

    span = group * tiles * blocks
    groups = half // group
    half_rows = half * tiles * blocks
    members = [(m, k) for m in range(group) for k in range(tiles)]

    def turned(n, g, v):
        return [
            turn(wd, 2 * v * blocks, n * half + g * group + m, v * tiles + k, 1)
            for m, k in members
        ]

    def keep_first(g, v, h):
        high, low = halves(h)
        for i, (m, k) in enumerate(members):
            rows = slice(i * blocks, (i + 1) * blocks)
            to = slice(v * blocks, (v + 1) * blocks)
            right[g * len(members) + i, to, :LANES] = high[rows, :]
            right[g * len(members) + i, to, LANES:] = low[rows, :]

    def keep_second(g, v, h):
        f[pl.ds(v * half_rows + g * span, span), :] = h

    def spread_views(g):
        for v in range(views):
            lhs = stacked(turned(0, g, v) + turned(1, g, v))
            h = jnp.dot(lhs, resp_t[v], preferred_element_type=jnp.float32)
            keep_first(g, v, h[:span, :])
            keep_second(g, v, h[span:, :])

    def mix_first(g):
        for i in range(len(members)):
            t = g * len(members) + i
            both = jnp.dot(
                couple[t, 0, :, :size], right[t, :size, :], preferred_element_type=jnp.float32
            )
            both = both + jnp.dot(
                couple[t, 1, :, :size], right[t, :size, :], preferred_element_type=jnp.float32
            )
            mixed = both[:, :LANES] + both[:, LANES:]
            high, low = halves(mixed)
            for w in range(views):
                rows = slice(w * blocks, (w + 1) * blocks)
                zs[w, i * blocks : (i + 1) * blocks, :LANES] = high[rows, :]
                zs[w, i * blocks : (i + 1) * blocks, LANES:] = low[rows, :]

    def mix_second(g, w, slot):
        for i, (m, k) in enumerate(members):
            total = None
            for v in range(views):
                here = f[pl.ds(g * span + v * half_rows + i * blocks, blocks), :]
                row = (g * group + m) * per_device + v * tiles + k
                row = (2 * row + w // half_views) * table_rows + w % half_views
                factor = coef[pl.ds(row, 8, stride=0), :]
                term = jnp.concatenate([factor] * (blocks // 8), axis=0) * here
                total = term if total is None else total + term
            high, low = halves(total)
            rows = slice(i * blocks, (i + 1) * blocks)
            slot[rows, :LANES] = high
            slot[rows, LANES:] = low

    def gather(n, g, w, slot, hd):
        h = jnp.dot(slot[...], resp[w], preferred_element_type=jnp.float32)
        for i in range(len(members)):
            part = h[i * blocks : (i + 1) * blocks, :]
            hd[2 * i * blocks : (2 * i + 1) * blocks, :] = part
            hd[(2 * i + 1) * blocks : (2 * i + 2) * blocks, :] = part
        total = gy[w * blocks : (w + 1) * blocks, :]
        for i, (m, k) in enumerate(members):
            device = n * half + g * group + m
            total = total + turn(hd, 2 * i * blocks, device, w * tiles + k, -1)
        gy[w * blocks : (w + 1) * blocks, :] = total

    def mix_and_gather(g):
        mix_first(g)
        for w in range(views):
            mix_second(g, w, z2.at[w % 4])
            gather(1, g, w, z2.at[w % 4], hds[w % 2])
            gather(0, g, w, zs.at[w], hds[2 + w % 2])

    def apply():
        gy[...] = jnp.zeros_like(gy)
        if groups == 1:
            spread_views(0)
            mix_and_gather(0)
        else:
            lax.fori_loop(0, groups, lambda g, carry: (spread_views(g), carry)[1], 0)
            lax.fori_loop(0, groups, lambda g, carry: (mix_and_gather(g), carry)[1], 0)

    start = meas[...] - (first[:size, :] + second[:size, :])
    y[...] = start
    double(start)
    zero = jnp.zeros_like(start)
    d[...] = zero
    gd[...] = zero
    step[...] = zero
    for t in range(half * tiles):
        right[t, size:, :] = jnp.zeros((2 * LANES - size, 2 * LANES), jnp.bfloat16)

    def broadcast_one(device, carry):
        here = second[pl.ds(pl.multiple_of(size + device * table_rows, 8), table_rows), :]
        for c in range(per_device):
            for side in range(2):
                rows = pl.multiple_of((2 * (device * per_device + c) + side) * table_rows, 8)
                lane_of = side * (LANES // 2) + c
                coef[pl.ds(rows, table_rows), :] = jnp.broadcast_to(
                    here[:, lane_of : lane_of + 1], here.shape
                )
        return carry

    lax.fori_loop(0, half, broadcast_one, 0)
    to_scalars.wait()

    def iterate(n, norm_before):
        apply()
        new_y, new_gy = y[...], gy[...]
        norm = jnp.sum(new_y * new_gy)
        beta = jnp.where(n == 0, 0.0, norm / norm_before)
        new_d = new_y + beta * d[...]
        new_gd = new_gy + beta * gd[...]
        product = jnp.sum(new_gd * new_gd) + jnp.sum(new_d * new_gd) / TAU_STEP
        alpha = norm / product
        d[...] = new_d
        gd[...] = new_gd
        step[...] = step[...] + alpha * new_d
        new_y = new_y - alpha * (new_gd + new_d / TAU_STEP)
        y[...] = new_y
        double(new_y)
        return norm

    lax.fori_loop(0, CG_ITERS, iterate, jnp.float32(1.0))

    double(step[...])
    own = tiles * blocks
    for v in range(views):
        lhs = stacked(
            [
                pull(
                    lambda q: wd[pl.ds(2 * v * blocks + q, blocks), :],
                    bins[k, angles[0, v]], lane,
                )
                for k in range(tiles)
            ]
        )
        fs[v * own : (v + 1) * own, :] = jnp.dot(
            lhs, resp_t[v], preferred_element_type=jnp.float32
        )
    for b in range(0, blocks, 2):
        picked = [fs[pl.ds(b + n, views * tiles, stride=blocks), :] for n in range(2)]
        here = slice(b * LANES, (b + 2) * LANES)
        out[:, here] = (
            image[:, here]
            - TAU_STEP * (behind[:, here] - dual_new[:, here])
            + product(spread[...], jnp.concatenate(picked, axis=1))
        )


VMEM = pl.BlockSpec(memory_space=pltpu.VMEM)
SMEM = pl.BlockSpec(memory_space=pltpu.SMEM)
PLACE = pl.BlockSpec(memory_space=pl.ANY)


def f32(*shape):
    return pltpu.VMEM(shape, jnp.float32)


def stay(x):
    return pltpu.with_memory_space_constraint(x, pltpu.MemorySpace.HBM)


def kernel(body, out_shape, scalars, arrays, scratch=(), limit=16 << 20, in_place=()):
    single = not isinstance(out_shape, tuple)
    return pl.pallas_call(
        body,
        out_shape=out_shape,
        in_specs=[SMEM] * len(scalars) + [VMEM] * len(arrays) + [PLACE] * len(in_place),
        out_specs=VMEM if single else (VMEM,) * len(out_shape),
        scratch_shapes=list(scratch),
        compiler_params=pltpu.CompilerParams(vmem_limit_bytes=limit),
    )(
        *(stay(a) if lies else a for a, lies in scalars),
        *(pltpu.with_memory_space_constraint(a, pltpu.MemorySpace.VMEM) for a in arrays),
        *map(stay, in_place),
    )


def exchange(x, sizes, ahead, mask):
    phases, rows = sizes
    pairs = [
        (t * rows + r, ((t + ahead) % phases) * rows + (r ^ mask))
        for t in range(phases)
        for r in range(rows)
    ]
    return lax.ppermute(x, ("tm", "row"), pairs)


def local(image, relaxed, dual, sinogram, angle_index, bin_offset, row_weight, response, row_gain):
    phases, devices = lax.axis_size("tm"), lax.axis_size("row")
    sizes = (phases, devices)
    num_rows, cols = image.shape[2:]
    views = angle_index.shape[1]
    tiles = bin_offset.shape[0]
    blocks = cols // LANES
    size = views * blocks
    image2, relaxed2, dual2 = (a.reshape(num_rows, cols) for a in (image, relaxed, dual))

    ring = [(i, (i - 1) % phases) for i in range(phases)]
    next_angles = lax.ppermute(angle_index, "tm", ring)
    ahead = lax.ppermute(relaxed2, "tm", ring)

    gain = row_gain.reshape(1, num_rows)
    meas = sinogram.reshape(size, LANES)
    table_rows = -(-(views // 2 + 1) // 8) * 8
    assert views % 2 == 0 and tiles * views <= LANES // 2
    dims = dict(tiles=tiles, views=views, blocks=blocks)
    twice = pltpu.VMEM((views, 2 * LANES, LANES), jnp.bfloat16)
    spreads = f32(views * tiles, num_rows)
    tall = pltpu.VMEM((row_weight.shape[0], num_rows), jnp.float32)

    own_angles, offsets = (angle_index, True), (bin_offset, True)
    resp, resp_t, spread, spread_t, table, before, rest, gained = kernel(
        functools.partial(own_kernel, **dims),
        (
            twice, twice, spreads, f32(num_rows, views * tiles), f32(table_rows, LANES),
            f32(size, LANES), f32(num_rows, cols), tall,
        ),
        (own_angles, offsets),
        (),
        project_scratch(1, **dims)
        + [
            pltpu.VMEM((-(-views // 8) * 8, num_rows), jnp.float32),
            pltpu.VMEM(row_weight.shape[::-1], jnp.float32),
            pltpu.VMEM(gain.shape, jnp.float32),
            pltpu.VMEM((3, num_rows, cols), jnp.float32),
            pltpu.SemaphoreType.DMA((2 * views + 5,)),
        ],
        in_place=(row_weight.T, gain, image2, dual2, relaxed2, response),
    )
    resp_next, spread_next = kernel(
        functools.partial(next_kernel, tiles=tiles, views=views),
        (twice, spreads),
        ((next_angles, False),),
        (gained,),
        [pltpu.SemaphoreType.DMA((2 * views,))],
        in_place=(response,),
    )
    dual_new, msg, msg_next = kernel(
        functools.partial(dual_kernel, **dims),
        (f32(num_rows, cols), f32(size + table_rows, LANES), f32(size, LANES)),
        (own_angles, (next_angles, False), offsets),
        (rest, ahead, spread, spread_next, resp, resp_next, before, table),
        project_scratch(2, **dims),
    )

    masks = [1 << b if b < 2 else 3 << (b - 1) for b in range(devices.bit_length() - 1)]
    masks = masks[:1] + masks[:0:-1]
    got = exchange(msg, sizes, 0, masks[0])
    got_next = exchange(msg_next, sizes, 1, 0)
    got_cross = exchange(msg_next, sizes, 1, masks[0])
    total = msg[:size] + got[:size] + (got_next + got_cross)
    tables = jnp.concatenate([msg[size:], got[size:]], axis=0)
    for mask in masks[1:]:
        msg = jnp.concatenate([total, tables], axis=0)
        got = exchange(msg, sizes, 0, mask)
        total = msg[:size] + got[:size]
        tables = jnp.concatenate([msg[size:], got[size:]], axis=0)
    half = devices // 2
    couple = kernel(
        functools.partial(couple_kernel, size=size, table_rows=table_rows, **dims),
        pltpu.VMEM((half * tiles, 2, size, 2 * LANES), jnp.bfloat16),
        (),
        (msg,),
        [pltpu.VMEM((4 * half * tiles * table_rows, 2 * LANES), jnp.float32)],
        limit=(4 << 20) + half * tiles * (4 * table_rows * 2 * LANES * 4),
    )
    behind = lax.ppermute(dual_new, "tm", [(i, (i + 1) % phases) for i in range(phases)])

    group = max(1, 16 // tiles)
    while half % group:
        group //= 2
    whole = half * tiles * blocks
    span = group * tiles * blocks
    image_new = kernel(
        functools.partial(
            cg_kernel, **dims, devices=devices, group=group, table_rows=table_rows
        ),
        jax.ShapeDtypeStruct((num_rows, cols), jnp.float32),
        (own_angles, offsets),
        (couple, msg, got, meas, resp, resp_t, spread_t, image2, dual_new, behind),
        [pltpu.VMEM((size, LANES), jnp.float32)] * 5
        + [
            pltpu.VMEM((2 * size, LANES), jnp.float32),
            pltpu.VMEM((views * whole, LANES), jnp.float32),
            pltpu.VMEM((half * tiles, 2 * LANES, 2 * LANES), jnp.bfloat16),
            pltpu.VMEM((4, span, 2 * LANES), jnp.bfloat16),
            pltpu.VMEM((views, span, 2 * LANES), jnp.bfloat16),
        ]
        + [pltpu.VMEM((2 * span, LANES), jnp.float32)] * 4
        + [
            pltpu.VMEM((views * tiles * blocks, LANES), jnp.float32),
            pltpu.VMEM((2 * half * tiles * views * table_rows, LANES), jnp.float32),
            pltpu.VMEM((4 * devices, LANES), jnp.int32),
            pltpu.SMEM((4 * devices, LANES), jnp.int32),
            pltpu.SemaphoreType.DMA,
        ],
        limit=(12 << 20) + 14 * views * whole * LANES,
    )
    return image_new.reshape(image.shape), dual_new.reshape(dual.shape)


def solution(mesh):
    return jax.shard_map(
        local,
        mesh=mesh,
        in_specs=(
            P("tm", None, "row", None),
            P("tm", None, "row", None),
            P("tm", None, "row", None),
            P("tm", None, None, None),
            P("tm", None),
            P("row", None),
            P(),
            P(),
            P("row"),
        ),
        out_specs=(P("tm", None, "row", None), P("tm", None, "row", None)),
        check_vma=False,
    )
```
